32 devices in a mesh: ctx: 4 (over z), fsdp: 8 (over y, x, core).
Axes of the slice: x: 2, y: 2, z: 4, core: 2. Of those that a mesh axis runs over, the one named last changes fastest.
Arguments:
- tokens: bfloat16 [8, 512, 1024], P('fsdp', 'ctx'), may hold values from -12 to 12
- cotangent: bfloat16 [8, 512, 1024], P('fsdp', 'ctx'), may hold values from -6 to 6
- weight_rows: float32 [12288, 1024], P('fsdp'), may hold values from -2 to 2
- first_rows: float32 [12288, 1024], P('fsdp')
- second_rows: float32 [12288, 1024], P('fsdp'), as said below
- vector_rows: float32 [12, 1024], replicated, may hold values from -2 to 2
- vector_first: float32 [12, 1024], replicated
- vector_second: float32 [12, 1024], replicated, as said below
Outputs:
- output: bfloat16 [8, 512, 1024], P('fsdp', 'ctx')
- input_grad: float32 [8, 512, 1024], P('fsdp', 'ctx')
- weight_grad: float32 [12288, 1024], P('fsdp')
- new_weights: float32 [12288, 1024], P('fsdp')
- new_first: float32 [12288, 1024], P('fsdp')
- new_second: float32 [12288, 1024], P('fsdp')
- vector_grad: float32 [12, 1024], replicated
- new_vectors: float32 [12, 1024], replicated
- new_vector_first: float32 [12, 1024], replicated
- new_vector_second: float32 [12, 1024], replicated
The draws below stay inside these ranges and needn't reach their ends.
Inputs may be any that keep to these rules, and one draw needn't show every extreme that they name: `second_rows`: every entry is positive. `vector_second`: every entry is positive.
All inputs are finite; a program needn't handle non-finite values.
Results may differ from the reference program's by a relative error of at most 0.025.
The reference program's roundings to bfloat16 on the way count: a program that leaves them out, or rounds other values in their place, can miss the bound.
Values may be sent and summed in bfloat16 or wider, within the bound.
No kernel may reach another device: no remote copies, remote signals or barrier semaphores. Data moves between devices by JAX's collectives and lax.ppermute only.
A program may use at most 320 MiB of HBM per device.

```python
import math
import jax
import jax.numpy as jnp
from jax import lax

D = 1024
HEADS = 16
FF = 4096
HEAD_DIM = 64
LENGTH = 512
SEQS = 8
ROWS = 12288
VROWS = 12


def draw_tokens(key, part):
    keys = jax.random.split(jax.random.fold_in(key, 7), 1)
    layout = (SEQS, LENGTH, D)
    result = jnp.clip(jax.random.normal(keys[0], layout, jnp.float32), -6.0, 6.0)
    return jnp.clip(result, -12.0, 12.0).astype(jnp.bfloat16)


def rough_values(key, layout, spread):
    return spread * jnp.clip(jax.random.normal(key, layout, jnp.float32), -4.0, 4.0)


def draw_weight_rows(key, part):
    keys = jax.random.split(jax.random.fold_in(key, 11), 6)
    width_inv = 1.0 / math.sqrt(D)
    query_t = rough_values(keys[0], (D, D), math.sqrt(2.0) * width_inv)
    key_t = rough_values(keys[1], (D, D), math.sqrt(2.0) * width_inv)
    value_t = rough_values(keys[2], (D, D), width_inv)
    out_t = rough_values(keys[3], (D, D), 3.0 * width_inv)
    up_t = rough_values(keys[4], (FF, D), width_inv)
    down_w = rough_values(keys[5], (FF, D), 1.5 / math.sqrt(FF))
    return jnp.concatenate([query_t, key_t, value_t, out_t, up_t, down_w], axis=0)


def draw_vector_rows(key, part):
    keys = jax.random.split(jax.random.fold_in(key, 13), 9)
    rows = [rough_values(keys[0], (D,), 0.5), rough_values(keys[1], (D,), 0.5), rough_values(keys[2], (D,), 0.3), 1.0 + rough_values(keys[3], (D,), 0.15), rough_values(keys[4], (D,), 0.3), rough_values(keys[5], (D,), 0.3), 1.0 + rough_values(keys[6], (D,), 0.15), rough_values(keys[7], (D,), 0.3)]
    small = jnp.stack(rows)
    bias_rows = rough_values(keys[8], (FF // D, D), 0.5)
    return jnp.concatenate([small, bias_rows], axis=0)


def first_values(key, layout):
    return rough_values(key, layout, 0.02 * math.sqrt(SEQS * LENGTH))


def second_values(key, layout):
    lowest = SEQS * LENGTH / 20000.0
    exponent = jax.random.uniform(key, layout, jnp.float32, 0.0, math.log(10.0))
    return lowest * jnp.exp(exponent)


def draw_first_rows(key, part):
    return first_values(jax.random.fold_in(key, 23), (ROWS, D))


def draw_second_rows(key, part):
    return second_values(jax.random.fold_in(key, 37), (ROWS, D))


def draw_vector_first(key, part):
    return first_values(jax.random.fold_in(key, 41), (VROWS, D))


def draw_vector_second(key, part):
    return second_values(jax.random.fold_in(key, 43), (VROWS, D))


def block_levels(stream_key, shape, cuts, least, high):
    level, own = 1.0, jax.random.fold_in(stream_key, 6)
    for axis_at, parts in cuts:
        steps = jnp.exp(jax.random.uniform(jax.random.fold_in(own, axis_at), (parts,), jnp.float32, least / len(cuts), high / len(cuts)))
        level = level * jnp.repeat(steps, shape[axis_at] // parts).reshape([-1 if axis == axis_at else 1 for axis in range(len(shape))])
    return level


def gaussian(rng, extent, scale, reach, shards=(), kind=jnp.bfloat16):
    array = scale * jax.random.normal(rng, extent, jnp.float32)
    if shards:
        array = array * block_levels(rng, extent, shards, -0.22, 0.18)
    return jnp.clip(array, -reach, reach).astype(kind)


def setup_inputs(seed: int = 0) -> dict:
    splits = jax.random.split(jax.random.key(seed), 9)
    tokens = draw_tokens(jax.random.fold_in(splits[8], 71), 0)
    cotangent = gaussian(splits[1], (SEQS, LENGTH, D), 1.0, 6.0, ((0, 8), (1, 4)))
    weight_rows = draw_weight_rows(jax.random.fold_in(splits[8], 71), 0)
    first_rows = draw_first_rows(jax.random.fold_in(splits[8], 71), 0)
    second_rows = draw_second_rows(jax.random.fold_in(splits[8], 71), 0)
    vector_rows = draw_vector_rows(jax.random.fold_in(splits[8], 71), 0)
    vector_first = draw_vector_first(jax.random.fold_in(splits[8], 71), 0)
    vector_second = draw_vector_second(jax.random.fold_in(splits[8], 71), 0)
    return dict(tokens=tokens, cotangent=cotangent, weight_rows=weight_rows, first_rows=first_rows, second_rows=second_rows, vector_rows=vector_rows, vector_first=vector_first, vector_second=vector_second)


beta_one = 0.9
beta_two = 0.999
learn_rate = 0.01
decay_rate = 0.01
adam_eps = 1e-08
norm_eps = 1e-05
adam_step = 2

def mat_nt(left, right):
    return lax.dot_general(left, right, (((1,), (1,)), ((), ())), preferred_element_type=jnp.float32)

def mat_tn(left, right):
    return lax.dot_general(left, right, (((0,), (0,)), ((), ())), preferred_element_type=jnp.float32)

def unpack(rows, vectors):
    width = rows.shape[1]
    hidden = (rows.shape[0] - 4 * width) // 2
    return [rows[:3 * width], vectors[0], vectors[1], rows[3 * width:4 * width], vectors[2], vectors[3], vectors[4], rows[4 * width:4 * width + hidden], vectors[8:].reshape(hidden), rows[4 * width + hidden:], vectors[5], vectors[6], vectors[7]]

def normalize(values):
    centred = values - lax.optimization_barrier(jnp.mean(values, axis=-1, keepdims=True))
    inverse = lax.rsqrt(lax.optimization_barrier(jnp.mean(centred * centred, axis=-1, keepdims=True)) + norm_eps)
    return (centred * inverse, inverse)

def norm_back(grad_norm, normed, inverse):
    return inverse * (grad_norm - lax.optimization_barrier(jnp.mean(grad_norm, axis=-1, keepdims=True)) - normed * lax.optimization_barrier(jnp.mean(grad_norm * normed, axis=-1, keepdims=True)))

def gelu_grad(pre_act):
    return 0.5 * (1.0 + lax.erf(pre_act * 0.7071067811865476)) + pre_act * jnp.exp(-0.5 * pre_act * pre_act) * 0.3989422804014327

def project(inputs, params):
    qkv_t, query_b, value_b = (params[0], params[1], params[2])
    width = qkv_t.shape[1]
    projected = mat_nt(inputs, qkv_t)
    query_rows = (projected[:, :width] + query_b.astype(jnp.float32)).astype(jnp.bfloat16)
    key_rows = projected[:, width:2 * width].astype(jnp.bfloat16)
    value_rows = (projected[:, 2 * width:] + value_b.astype(jnp.float32)).astype(jnp.bfloat16)
    return (query_rows, key_rows, value_rows)

def tail_forward(inputs, attended, params):
    out_t, out_b, gain_one, shift_one, up_t, up_b, down_w, down_b, gain_two, shift_two = params[3:]
    first_sum = inputs.astype(jnp.float32) + mat_nt(attended, out_t) + out_b.astype(jnp.float32)
    normed_one, inverse_one = normalize(first_sum)
    hidden_in = normed_one * gain_one.astype(jnp.float32) + shift_one.astype(jnp.float32)
    hidden_b = hidden_in.astype(jnp.bfloat16)
    pre_act = mat_nt(hidden_b, up_t) + up_b.astype(jnp.float32)
    activ_b = jax.nn.gelu(pre_act, approximate=False).astype(jnp.bfloat16)
    second_sum = hidden_in + jnp.dot(activ_b, down_w, preferred_element_type=jnp.float32) + down_b.astype(jnp.float32)
    normed_two, inverse_two = normalize(second_sum)
    output = (normed_two * gain_two.astype(jnp.float32) + shift_two.astype(jnp.float32)).astype(jnp.bfloat16)
    return (output, (normed_one, inverse_one, hidden_b, pre_act, activ_b, normed_two, inverse_two))

def tail_backward(cotan, attended, saved, params):
    out_t, out_b, gain_one, shift_one, up_t, up_b, down_w, down_b, gain_two, shift_two = params[3:]
    normed_one, inverse_one, hidden_b, pre_act, activ_b, normed_two, inverse_two = saved
    grad_gain_two = lax.optimization_barrier(jnp.sum(cotan * normed_two, axis=0))
    grad_shift_two = lax.optimization_barrier(jnp.sum(cotan, axis=0))
    grad_second = norm_back(cotan * gain_two.astype(jnp.float32), normed_two, inverse_two)
    grad_second_b = grad_second.astype(jnp.bfloat16)
    grad_down_b = lax.optimization_barrier(jnp.sum(grad_second, axis=0))
    grad_down_w = mat_tn(activ_b, grad_second_b)
    grad_pre = mat_nt(grad_second_b, down_w) * gelu_grad(pre_act)
    grad_pre_b = grad_pre.astype(jnp.bfloat16)
    grad_up_b = lax.optimization_barrier(jnp.sum(grad_pre, axis=0))
    grad_up_t = mat_tn(grad_pre_b, hidden_b)
    grad_hidden = grad_second + jnp.dot(grad_pre_b, up_t, preferred_element_type=jnp.float32)
    grad_gain_one = lax.optimization_barrier(jnp.sum(grad_hidden * normed_one, axis=0))
    grad_shift_one = lax.optimization_barrier(jnp.sum(grad_hidden, axis=0))
    grad_first = norm_back(grad_hidden * gain_one.astype(jnp.float32), normed_one, inverse_one)
    grad_first_b = grad_first.astype(jnp.bfloat16)
    grad_out_b = lax.optimization_barrier(jnp.sum(grad_first, axis=0))
    grad_out_t = mat_tn(grad_first_b, attended)
    grad_attended = jnp.dot(grad_first_b, out_t, preferred_element_type=jnp.float32).astype(jnp.bfloat16)
    tail_grads = (grad_out_t, grad_out_b, grad_gain_one, grad_shift_one, grad_up_t, grad_up_b, grad_down_w, grad_down_b, grad_gain_two, grad_shift_two)
    return (grad_first, grad_attended, tail_grads)

def head_backward(inputs, grad_first, grad_query, grad_key, grad_value, qkv_t):
    grad_proj_b = jnp.concatenate([grad_query, grad_key, grad_value], axis=1).astype(jnp.bfloat16)
    grad_qkv_t = mat_tn(grad_proj_b, inputs)
    grad_inputs = grad_first + jnp.dot(grad_proj_b, qkv_t, preferred_element_type=jnp.float32)
    return (grad_inputs, grad_qkv_t, lax.optimization_barrier(jnp.sum(grad_query, axis=0)), lax.optimization_barrier(jnp.sum(grad_value, axis=0)))

def pack_grads(grad_qkv_t, grad_query_b, grad_value_b, tail_grads):
    width = grad_qkv_t.shape[1]
    matrix = jnp.concatenate([grad_qkv_t, tail_grads[0], tail_grads[4], tail_grads[6]], axis=0)
    small = jnp.stack([grad_query_b, grad_value_b, tail_grads[1], tail_grads[2], tail_grads[3], tail_grads[7], tail_grads[8], tail_grads[9]])
    vectors = jnp.concatenate([small, tail_grads[5].reshape(-1, width)], axis=0)
    return (matrix, vectors)

def adam_update(weights, grads, first, second):
    first_new = beta_one * first + (1.0 - beta_one) * grads
    second_new = beta_two * second + (1.0 - beta_two) * grads * grads
    first_hat = first_new / (1.0 - beta_one ** adam_step)
    second_hat = second_new / (1.0 - beta_two ** adam_step)
    weights_new = weights - learn_rate * (first_hat / (jnp.sqrt(second_hat) + adam_eps) + decay_rate * weights)
    return (weights_new, first_new, second_new)

def to_heads(matrix):
    return matrix.reshape(matrix.shape[0], HEADS, matrix.shape[1] // HEADS).transpose(1, 0, 2)

def from_heads(stacked):
    return stacked.transpose(1, 0, 2).reshape(stacked.shape[1], stacked.shape[0] * stacked.shape[2])

def attention_forward(query_rows, key_rows, value_rows):
    score_scale = 1.0 / math.sqrt(HEAD_DIM)

    def one_head(triple):
        query_h, key_h, value_h = triple
        scores = jnp.dot(query_h, key_h.T, preferred_element_type=jnp.float32) * score_scale
        row_top = lax.optimization_barrier(jnp.max(scores, axis=-1, keepdims=True))
        log_total = row_top + jnp.log(lax.optimization_barrier(jnp.sum(jnp.exp(scores - row_top), axis=-1, keepdims=True)))
        probs = jnp.exp(scores - log_total)
        result = jnp.dot(probs, value_h.astype(jnp.float32), precision=lax.Precision.HIGHEST)
        return (result, log_total[:, 0])
    out_heads, log_totals = lax.map(one_head, (to_heads(query_rows), to_heads(key_rows), to_heads(value_rows)))
    return (from_heads(out_heads).astype(jnp.bfloat16), log_totals)

def attention_backward(query_rows, key_rows, value_rows, attended, grad_attended, log_totals):
    score_scale = 1.0 / math.sqrt(HEAD_DIM)

    def one_head(items):
        query_h, key_h, value_h, attended_h, grad_h, log_total = items
        scores = jnp.dot(query_h, key_h.T, preferred_element_type=jnp.float32) * score_scale
        probs = jnp.exp(scores - log_total[:, None])
        delta = lax.optimization_barrier(jnp.sum(grad_h.astype(jnp.float32) * attended_h.astype(jnp.float32), axis=-1))
        grad_probs = jnp.dot(grad_h, value_h.T, preferred_element_type=jnp.float32)
        grad_scores = (probs * (grad_probs - delta[:, None])).astype(jnp.bfloat16)
        probs_b = probs.astype(jnp.bfloat16)
        grad_query = jnp.dot(grad_scores, key_h, preferred_element_type=jnp.float32) * score_scale
        grad_key = jnp.dot(grad_scores.T, query_h, preferred_element_type=jnp.float32) * score_scale
        grad_value = jnp.dot(probs_b.T, grad_h, preferred_element_type=jnp.float32)
        return (grad_query, grad_key, grad_value)
    stacked = (to_heads(query_rows), to_heads(key_rows), to_heads(value_rows), to_heads(attended), to_heads(grad_attended), log_totals)
    grad_query, grad_key, grad_value = lax.map(one_head, stacked)
    return (from_heads(grad_query), from_heads(grad_key), from_heads(grad_value))

def reference(tokens, cotangent, weight_rows, first_rows, second_rows, vector_rows, vector_first, vector_second):
    params = unpack(weight_rows.astype(jnp.bfloat16), vector_rows.astype(jnp.bfloat16))

    def per_sequence(sums, items):
        matrix_sum, vector_sum = sums
        inputs, cotan_b = items
        query_rows, key_rows, value_rows = project(inputs, params)
        attended, log_totals = attention_forward(query_rows, key_rows, value_rows)
        output, saved = tail_forward(inputs, attended, params)
        grad_first, grad_attended, tail_grads = tail_backward(cotan_b.astype(jnp.float32), attended, saved, params)
        grad_query, grad_key, grad_value = attention_backward(query_rows, key_rows, value_rows, attended, grad_attended, log_totals)
        grad_inputs, grad_qkv_t, grad_query_b, grad_value_b = head_backward(inputs, grad_first, grad_query, grad_key, grad_value, params[0])
        matrix, vectors = pack_grads(grad_qkv_t, grad_query_b, grad_value_b, tail_grads)
        return ((matrix_sum + matrix, vector_sum + vectors), (output, grad_inputs))
    start = (jnp.zeros(weight_rows.shape, jnp.float32), jnp.zeros(vector_rows.shape, jnp.float32))
    (matrix_total, vector_total), (outputs, grad_inputs) = lax.scan(per_sequence, start, (tokens, cotangent))
    new_weights, new_first, new_second = adam_update(weight_rows, matrix_total, first_rows, second_rows)
    new_vectors, new_vfirst, new_vsecond = adam_update(vector_rows, vector_total, vector_first, vector_second)
    return (outputs, grad_inputs, matrix_total, new_weights, new_first, new_second, vector_total, new_vectors, new_vfirst, new_vsecond)
```

```python
import math

import jax
import jax.numpy as jnp
from jax import lax
from jax.sharding import PartitionSpec as P

D = 1024
HEADS = 16
HEAD_DIM = D // HEADS

beta_one = 0.9
beta_two = 0.999
learn_rate = 0.01
decay_rate = 0.01
adam_eps = 1e-08
norm_eps = 1e-05
adam_step = 2

f32 = jnp.float32
bf16 = jnp.bfloat16


def mat_nt(left, right):
    return lax.dot_general(left, right, (((1,), (1,)), ((), ())), preferred_element_type=f32)


def mat_tn(left, right):
    return lax.dot_general(left, right, (((0,), (0,)), ((), ())), preferred_element_type=f32)


def mat_nn(left, right):
    return jnp.dot(left, right, preferred_element_type=f32)


def normalize(values):
    centred = values - jnp.mean(values, axis=-1, keepdims=True)
    inverse = lax.rsqrt(jnp.mean(centred * centred, axis=-1, keepdims=True) + norm_eps)
    return (centred * inverse, inverse)


def norm_back(grad_norm, normed, inverse):
    return inverse * (
        grad_norm
        - jnp.mean(grad_norm, axis=-1, keepdims=True)
        - normed * jnp.mean(grad_norm * normed, axis=-1, keepdims=True)
    )


def adam_update(weights, grads, first, second):
    first_new = beta_one * first + (1.0 - beta_one) * grads
    second_new = beta_two * second + (1.0 - beta_two) * grads * grads
    first_hat = first_new / (1.0 - beta_one**adam_step)
    second_hat = second_new / (1.0 - beta_two**adam_step)
    weights_new = weights - learn_rate * (
        first_hat / (jnp.sqrt(second_hat) + adam_eps) + decay_rate * weights
    )
    return (weights_new, first_new, second_new)


def at(array, index, axis=0):
    return lax.dynamic_index_in_dim(array, index, axis, keepdims=False)


def local(
    tokens,
    cotangent,
    weight_rows,
    first_rows,
    second_rows,
    vector_rows,
    vector_first,
    vector_second,
):
    C = lax.axis_size("ctx")
    F = lax.axis_size("fsdp")
    K = F // C
    z = lax.axis_index("ctx")
    f = lax.axis_index("fsdp")
    g = f // K
    c = f % K
    T = tokens.shape[1]
    own_rows = weight_rows.shape[0]
    total_rows = own_rows * F
    hidden = (total_rows - 4 * D) // 2
    B = math.gcd(own_rows, D)
    direct = (B // C) % HEAD_DIM == 0
    if not direct:
        B = D
    s = B // C
    per = D // B
    nb = own_rows // B if direct else 0
    blocks = total_rows // B
    first_o, last_o = 3 * per, 4 * per

    swap_pairs = [
        (zz * F + K * gg + cc, gg * F + K * zz + cc)
        for zz in range(C)
        for gg in range(C)
        for cc in range(K)
    ]

    def swap(array):
        return lax.ppermute(array, ("ctx", "fsdp"), swap_pairs)

    def hop(array, d):
        return lax.ppermute(array, "fsdp", [(i, K * ((i // K) ^ d) + i % K) for i in range(F)])

    def gather(block):
        return jnp.concatenate([block] + [hop(block, d) for d in range(1, C)], axis=0)

    def scatter(partial):
        parts = partial.reshape(C, T, D)
        sent = parts.astype(bf16)
        total = parts[0]
        for d in range(1, C):
            total = total + hop(sent[d], d).astype(f32)
        return total

    def cores(array, k):
        return lax.ppermute(array, "fsdp", [(i, K * (i // K) + (i + k) % K) for i in range(F)])

    ring_pairs = [(i, (i + 1) % C) for i in range(C)]

    def ring_scatter(parts):
        total = at(parts, (z + C - 1) % C)
        for step in range(C - 1):
            arrived = lax.ppermute(total.astype(bf16), "ctx", ring_pairs)
            total = arrived.astype(f32) + at(parts, (z + 2 * C - 2 - step) % C)
        return total

    def ring_gather(block):
        held = [block]
        for _ in range(C - 1):
            held.append(lax.ppermute(held[-1], "ctx", ring_pairs))
        held = jnp.stack(held)
        return [at(held, (z + C - zz) % C) for zz in range(C)]

    def row_form(rows):
        return rows.reshape(-1, C, s, D)

    def column_form(rows):
        n = rows.shape[0] // B
        return rows.reshape(n, C, s, per, C, s).transpose(0, 4, 2, 1, 3, 5).reshape(n, C, s, D)

    def from_column_form(blocks_):
        n = blocks_.shape[0]
        return blocks_.reshape(n, C, s, C, per, s).transpose(0, 3, 2, 4, 1, 5).reshape(n, B, D)

    block_ids = nb * f + jnp.arange(max(nb, 1))
    is_o = ((block_ids >= first_o) & (block_ids < last_o))[:, None, None, None]

    weights_b = weight_rows.astype(bf16)
    if direct:
        payload = jnp.where(is_o, column_form(weights_b), row_form(weights_b))
        parts = [at(payload, g, 1)]
        for d in range(1, C):
            parts.append(hop(at(payload, g ^ d, 1), d))
        mine = jnp.stack(parts)
        both = jnp.stack([mine] + [cores(mine, k) for k in range(1, K)])
        slices = jnp.concatenate(
            [at(at(both, (c - cc) % K), gg ^ g) for gg in range(C) for cc in range(K)], axis=0
        )
    else:
        full = lax.all_gather(weights_b, "fsdp", axis=0, tiled=True)
        rows_part = at(row_form(full), g, 1)
        cols_part = at(column_form(full), g, 1)
        slices = jnp.concatenate(
            [rows_part[:first_o], cols_part[first_o:last_o], rows_part[last_o:]], axis=0
        )
    part = D // C
    w_qkv = slices[:first_o].reshape(3 * part, D)
    w_o = (
        slices[first_o:last_o]
        .reshape(per, s, C, per, s)
        .transpose(0, 2, 1, 3, 4)
        .reshape(D, part)
    )
    up_end = last_o + hidden // B
    w_1 = slices[last_o:up_end].reshape(hidden // C, D)
    w_2 = slices[up_end:].reshape(hidden // C, D)

    vectors = vector_rows.astype(bf16).astype(f32)

    def own_features(vector):
        return at(vector.reshape(-1, C, s), g, 1).reshape(-1)

    def place_features(vector, count):
        spread = jnp.zeros((count // B, C, s), f32)
        return lax.dynamic_update_slice(
            spread, vector.reshape(count // B, 1, s), (0, g, 0)
        ).reshape(count)

    query_b, value_b = own_features(vectors[0]), own_features(vectors[1])
    out_b, gain_one, shift_one, down_b, gain_two, shift_two = [vectors[i] for i in range(2, 8)]
    up_b = own_features(vectors[8:].reshape(hidden))

    inputs = swap(tokens.reshape(T, D))
    cotan = swap(cotangent.reshape(T, D)).astype(f32)
    sequence = gather(inputs)
    S = C * T
    heads = part // HEAD_DIM
    score_scale = 1.0 / math.sqrt(HEAD_DIM)

    def split_heads(matrix):
        return matrix.reshape(S, heads, HEAD_DIM).transpose(1, 0, 2)

    def join_heads(stacked):
        return stacked.transpose(1, 0, 2).reshape(S, part)

    def batched(spec, left, right):
        return jnp.einsum(spec, left, right, preferred_element_type=f32)

    projected = mat_nt(sequence, w_qkv)
    query = split_heads((projected[:, :part] + query_b).astype(bf16))
    key = split_heads(projected[:, part : 2 * part].astype(bf16))
    value = split_heads((projected[:, 2 * part :] + value_b).astype(bf16))
    scores = batched("hqd,hkd->hqk", query, key) * score_scale
    top = jnp.max(scores, axis=-1, keepdims=True)
    log_total = top + jnp.log(jnp.sum(jnp.exp(scores - top), axis=-1, keepdims=True))
    probs = jnp.exp(scores - log_total)
    probs_b = probs.astype(bf16)
    attended_h = batched("hqk,hkd->hqd", probs_b, value).astype(bf16)
    attended = join_heads(attended_h)

    first_sum = inputs.astype(f32) + scatter(mat_nt(attended, w_o)) + out_b
    normed_one, inverse_one = normalize(first_sum)
    hidden_in = normed_one * gain_one + shift_one
    hidden_all = gather(hidden_in.astype(bf16))
    pre_act = mat_nt(hidden_all, w_1) + up_b
    cdf = 0.5 * (1.0 + lax.erf(pre_act * 0.7071067811865476))
    activ_b = (pre_act * cdf).astype(bf16)
    second_sum = hidden_in + scatter(mat_nn(activ_b, w_2)) + down_b
    normed_two, inverse_two = normalize(second_sum)
    output = swap((normed_two * gain_two + shift_two).astype(bf16))

    grad_gain_two = jnp.sum(cotan * normed_two, axis=0)
    grad_shift_two = jnp.sum(cotan, axis=0)
    grad_second = norm_back(cotan * gain_two, normed_two, inverse_two)
    grad_down_b = jnp.sum(grad_second, axis=0)
    grad_second_all = gather(grad_second.astype(bf16))
    grad_down_w = mat_tn(activ_b, grad_second_all)
    gelu_grad = cdf + pre_act * jnp.exp(-0.5 * pre_act * pre_act) * 0.3989422804014327
    grad_pre = mat_nt(grad_second_all, w_2) * gelu_grad
    grad_up_b = jnp.sum(grad_pre, axis=0)
    grad_pre_b = grad_pre.astype(bf16)
    grad_hidden = grad_second + scatter(mat_nn(grad_pre_b, w_1))
    grad_up_w = mat_tn(grad_pre_b, hidden_all)
    grad_gain_one = jnp.sum(grad_hidden * normed_one, axis=0)
    grad_shift_one = jnp.sum(grad_hidden, axis=0)
    grad_first = norm_back(grad_hidden * gain_one, normed_one, inverse_one)
    grad_out_b = jnp.sum(grad_first, axis=0)
    grad_first_all = gather(grad_first.astype(bf16))
    grad_out_w = mat_tn(grad_first_all, attended)
    grad_att = split_heads(mat_nn(grad_first_all, w_o).astype(bf16))

    delta = jnp.sum(grad_att.astype(f32) * attended_h.astype(f32), axis=-1, keepdims=True)
    grad_probs = batched("hqd,hkd->hqk", grad_att, value)
    grad_scores = (probs * (grad_probs - delta)).astype(bf16)
    grad_query = join_heads(batched("hqk,hkd->hqd", grad_scores, key) * score_scale)
    grad_key = join_heads(batched("hqk,hqd->hkd", grad_scores, query) * score_scale)
    grad_value = join_heads(batched("hqk,hqd->hkd", probs_b, grad_att))
    grad_proj = jnp.concatenate([grad_query, grad_key, grad_value], axis=1).astype(bf16)
    grad_qkv_w = mat_tn(grad_proj, sequence)
    grad_inputs = swap((grad_first + scatter(mat_nn(grad_proj, w_qkv))).astype(bf16))

    small = jnp.stack(
        [
            place_features(jnp.sum(grad_query, axis=0), D),
            place_features(jnp.sum(grad_value, axis=0), D),
            grad_out_b,
            grad_gain_one,
            grad_shift_one,
            grad_down_b,
            grad_gain_two,
            grad_shift_two,
        ]
    )
    vector_total = jnp.concatenate(
        [small, place_features(grad_up_b, hidden).reshape(-1, D)], axis=0
    )
    vector_total = lax.psum(vector_total, ("ctx", "fsdp"))
    new_vectors, new_vfirst, new_vsecond = adam_update(
        vector_rows, vector_total, vector_first, vector_second
    )

    grad_blocks = jnp.concatenate(
        [
            grad_qkv_w.astype(bf16).reshape(3 * per, s, D),
            grad_out_w.astype(bf16)
            .reshape(per, C, s, per, s)
            .transpose(0, 2, 1, 3, 4)
            .reshape(per, s, D),
            grad_up_w.astype(bf16).reshape(hidden // B, s, D),
            grad_down_w.astype(bf16).reshape(hidden // B, s, D),
        ],
        axis=0,
    )
    if direct:
        by_owner = grad_blocks.reshape(C, K, nb * s, D)
        total = at(by_owner, c, 1).astype(f32)
        for k in range(1, K):
            total = total + cores(at(by_owner, (c + k) % K, 1), k).astype(f32)
        parts = total.reshape(C, nb, C, s // C, D).transpose(2, 0, 1, 3, 4)
        reduced = ring_scatter(parts).astype(bf16)
        pieces = [at(reduced, g)]
        for d in range(1, C):
            pieces.append(hop(at(reduced, g ^ d), d))
        pieces = jnp.stack(pieces)
        ordered = jnp.stack([at(pieces, gg ^ g) for gg in range(C)], axis=1)
        ordered = jnp.stack(ring_gather(ordered), axis=2)
        ordered = ordered.reshape(nb, C, s, D)
        grad_out = jnp.where(
            is_o.reshape(-1, 1, 1), from_column_form(ordered), ordered.reshape(nb, B, D)
        ).reshape(own_rows, D)
    else:
        spread = lax.dynamic_update_slice(
            jnp.zeros((blocks, C, s, D), bf16), grad_blocks[:, None], (0, g, 0, 0)
        )
        matrix = jnp.where(
            ((jnp.arange(blocks) >= first_o) & (jnp.arange(blocks) < last_o))[:, None, None],
            from_column_form(spread),
            spread.reshape(blocks, B, D),
        ).reshape(total_rows, D)
        grad_out = lax.psum_scatter(matrix, "fsdp", scatter_dimension=0, tiled=True)
        grad_out = lax.psum(grad_out, "ctx")
    grad_out = grad_out.astype(f32)
    weights_out, first_out, second_out = adam_update(weight_rows, grad_out, first_rows, second_rows)
    return (
        output.reshape(1, T, D),
        grad_inputs.astype(f32).reshape(1, T, D),
        grad_out,
        weights_out,
        first_out,
        second_out,
        vector_total,
        new_vectors,
        new_vfirst,
        new_vsecond,
    )


def solution(mesh):
    shared = P()
    rows = P("fsdp", None)
    blocks = P("fsdp", "ctx", None)
    return jax.shard_map(
        local,
        mesh=mesh,
        in_specs=(blocks, blocks, rows, rows, rows, shared, shared, shared),
        out_specs=(blocks, blocks, rows, rows, rows, rows, shared, shared, shared, shared),
        check_vma=False,
    )
```

```python
import math

import jax
import jax.numpy as jnp
from jax import lax
from jax.experimental import pallas as pl
from jax.experimental.pallas import tpu as pltpu
from jax.sharding import PartitionSpec as P

D = 1024
HEADS = 16
HEAD_DIM = D // HEADS

beta_one = 0.9
beta_two = 0.999
learn_rate = 0.01
decay_rate = 0.01
adam_eps = 1e-08
norm_eps = 1e-05
adam_step = 2

f32 = jnp.float32
bf16 = jnp.bfloat16


def mat_nt(left, right):
    return lax.dot_general(left, right, (((1,), (1,)), ((), ())), preferred_element_type=f32)


def mat_tn(left, right):
    return lax.dot_general(left, right, (((0,), (0,)), ((), ())), preferred_element_type=f32)


def mat_nn(left, right):
    return jnp.dot(left, right, preferred_element_type=f32)


def normalize(values):
    centred = values - jnp.mean(values, axis=-1, keepdims=True)
    inverse = lax.rsqrt(jnp.mean(centred * centred, axis=-1, keepdims=True) + norm_eps)
    return (centred * inverse, inverse)


def norm_back(grad_norm, normed, inverse):
    return inverse * (
        grad_norm
        - jnp.mean(grad_norm, axis=-1, keepdims=True)
        - normed * jnp.mean(grad_norm * normed, axis=-1, keepdims=True)
    )


def adam_update(weights, grads, first, second):
    first_new = beta_one * first + (1.0 - beta_one) * grads
    second_new = beta_two * second + (1.0 - beta_two) * grads * grads
    first_hat = first_new / (1.0 - beta_one**adam_step)
    second_hat = second_new / (1.0 - beta_two**adam_step)
    weights_new = weights - learn_rate * (
        first_hat / (jnp.sqrt(second_hat) + adam_eps) + decay_rate * weights
    )
    return (weights_new, first_new, second_new)


def at(array, index, axis=0):
    return lax.dynamic_index_in_dim(array, index, axis, keepdims=False)


def pack_kernel(C, s, per, nb, bounds, place, rows_ref, out_ref):
    slot = pl.program_id(1)
    owner = slot ^ place[0]
    block = nb * place[3] + pl.program_id(0)
    by_column = (block >= bounds[0]) & (block < bounds[1])

    @pl.when(jnp.logical_not(by_column))
    def _():
        start = pl.multiple_of(owner * s, s)
        out_ref[0, 0] = rows_ref[pl.ds(start, s), :].astype(bf16)

    @pl.when(by_column)
    def _():
        for m in range(C):
            for h in range(per):
                start = pl.multiple_of((h * C + owner) * s, s)
                to = (m * per + h) * s
                out_ref[0, 0, :, to : to + s] = rows_ref[
                    m * s : (m + 1) * s, pl.ds(start, s)
                ].astype(bf16)


def pack(place, rows, C, s, per, nb, bounds):
    width = rows.shape[1]
    return pl.pallas_call(
        lambda *refs: pack_kernel(C, s, per, nb, bounds, *refs),
        out_shape=jax.ShapeDtypeStruct((C, nb, s, width), bf16),
        grid_spec=pltpu.PrefetchScalarGridSpec(
            num_scalar_prefetch=1,
            grid=(nb, C),
            in_specs=[pl.BlockSpec((C * s, width), lambda b, d, place: (b, 0))],
            out_specs=pl.BlockSpec((1, 1, s, width), lambda b, d, place: (d, b, 0, 0)),
        ),
        name="pack",
    )(place, rows)


def unpack_kernel(K, nb, place, *refs):
    owner = pl.program_id(0) // nb
    core = owner % K
    out_ref = refs[-1]
    for k in range(K):

        @pl.when((place[1] + K - k) % K == core)
        def _(k=k):
            out_ref[...] = refs[k][0]


def unpack(place, pieces, C, K, s, nb):
    width = pieces[0].shape[-1]
    spec = pl.BlockSpec(
        (1, 1, s, width), lambda n, place: ((n // nb // K) ^ place[0], n % nb, 0, 0)
    )
    return pl.pallas_call(
        lambda *refs: unpack_kernel(K, nb, *refs),
        out_shape=jax.ShapeDtypeStruct((C * K * nb, s, width), bf16),
        grid_spec=pltpu.PrefetchScalarGridSpec(
            num_scalar_prefetch=1,
            grid=(C * K * nb,),
            in_specs=[spec] * K,
            out_specs=pl.BlockSpec((1, s, width), lambda n, place: (n, 0, 0)),
        ),
        name="unpack",
    )(place, *pieces)


def update_kernel(C, K, s, per, nb, bounds, place, *refs):
    by_row, by_col = refs[:K], refs[K : 2 * K]
    weights_ref, first_ref, second_ref = refs[2 * K : 2 * K + 3]
    grad_ref, weights_out, first_out, second_out = refs[2 * K + 3 :]
    g, c, z, f = place[0], place[1], place[2], place[3]
    block = nb * f + pl.program_id(0)
    by_column = (block >= bounds[0]) & (block < bounds[1])
    piece = s // K // C

    def start_of(k, e):
        return pl.multiple_of(((c + K - k) % K) * (s // K) + (z ^ e) * piece, piece)

    @pl.when(jnp.logical_not(by_column))
    def _():
        for k in range(K):
            for e in range(C):
                grad_ref[pl.ds(start_of(k, e), piece), :] = by_row[k][0, 0, e].astype(f32)

    @pl.when(by_column)
    def _():
        for k in range(K):
            for e in range(C):
                for d in range(C):
                    for h in range(per):
                        column = pl.multiple_of((h * C + (g ^ d)) * s, s)
                        grad_ref[pl.ds(start_of(k, e), piece), pl.ds(column, s)] = by_col[k][
                            d, 0, e, :, h * s : (h + 1) * s
                        ].astype(f32)

    new_weights, new_first, new_second = adam_update(
        weights_ref[...], grad_ref[...], first_ref[...], second_ref[...]
    )
    weights_out[...] = new_weights
    first_out[...] = new_first
    second_out[...] = new_second


def update(place, pieces, weights, first, second, C, K, s, per, nb, bounds):
    rows, width = weights.shape
    piece = s // K // C
    row_spec = pl.BlockSpec(
        (1, 1, C, piece, width), lambda b, m, place: (m ^ place[0], b, 0, 0, 0)
    )
    col_spec = pl.BlockSpec((C, 1, C, piece, per * s), lambda b, m, place: (0, b, 0, 0, m))
    tile = pl.BlockSpec((s, width), lambda b, m, place: (b * C + m, 0))
    whole = jax.ShapeDtypeStruct((rows, width), f32)
    return pl.pallas_call(
        lambda *refs: update_kernel(C, K, s, per, nb, bounds, *refs),
        out_shape=[whole] * 4,
        grid_spec=pltpu.PrefetchScalarGridSpec(
            num_scalar_prefetch=1,
            grid=(nb, C),
            in_specs=[row_spec] * K + [col_spec] * K + [tile] * 3,
            out_specs=[tile] * 4,
        ),
        name="update",
    )(place, *pieces, *pieces, weights, first, second)


def local(
    tokens,
    cotangent,
    weight_rows,
    first_rows,
    second_rows,
    vector_rows,
    vector_first,
    vector_second,
):
    C = lax.axis_size("ctx")
    F = lax.axis_size("fsdp")
    K = F // C
    z = lax.axis_index("ctx")
    f = lax.axis_index("fsdp")
    g = f // K
    c = f % K
    T = tokens.shape[1]
    own_rows = weight_rows.shape[0]
    total_rows = own_rows * F
    hidden = (total_rows - 4 * D) // 2
    B = math.gcd(own_rows, D)
    direct = (B // C) % HEAD_DIM == 0
    if not direct:
        B = D
    s = B // C
    per = D // B
    nb = own_rows // B if direct else 0
    blocks = total_rows // B
    first_o, last_o = 3 * per, 4 * per

    there = [
        (zz * F + K * gg + cc, gg * F + K * (zz ^ gg) + cc)
        for zz in range(C)
        for gg in range(C)
        for cc in range(K)
    ]
    back = [(to, source) for source, to in there]

    def swap(array):
        return lax.ppermute(array, ("ctx", "fsdp"), there)

    def swap_back(array):
        return lax.ppermute(array, ("ctx", "fsdp"), back)

    def hop(array, d):
        return lax.ppermute(array, "fsdp", [(i, K * ((i // K) ^ d) + i % K) for i in range(F)])

    def gather(block):
        return jnp.concatenate([block] + [hop(block, d) for d in range(1, C)], axis=0)

    def scatter(partial):
        parts = partial.reshape(C, T, D)
        sent = parts.astype(bf16)
        total = parts[0]
        for d in range(1, C):
            total = total + hop(sent[d], d).astype(f32)
        return total

    def cores(array, k):
        return lax.ppermute(array, "fsdp", [(i, K * (i // K) + (i + k) % K) for i in range(F)])

    def along(array, e):
        return lax.ppermute(array, "ctx", [(i, i ^ e) for i in range(C)])

    def all_sum(values):
        for axis, size in (("fsdp", F), ("ctx", C)):
            step = 1
            while step < size:
                values = values + lax.ppermute(
                    values, axis, [(i, i ^ step) for i in range(size)]
                )
                step *= 2
        return values

    def reduce_blocks(slices_):
        n = slices_.shape[0]
        parts = slices_.reshape(n, K, s // K, D)
        total = at(parts, c, 1)
        for k in range(1, K):
            total = total + cores(at(parts, (c + k) % K, 1).astype(bf16), k).astype(f32)
        total = total.reshape(n, C, s // K // C, D)
        summed = at(total, z, 1)
        for e in range(1, C):
            summed = summed + along(at(total, z ^ e, 1).astype(bf16), e).astype(f32)
        summed = summed.astype(bf16)
        return jnp.stack([summed] + [along(summed, e) for e in range(1, C)], axis=1)

    def row_form(rows):
        return rows.reshape(-1, C, s, D)

    def column_form(rows):
        n = rows.shape[0] // B
        return rows.reshape(n, C, s, per, C, s).transpose(0, 4, 2, 1, 3, 5).reshape(n, C, s, D)

    def from_column_form(blocks_):
        n = blocks_.shape[0]
        return blocks_.reshape(n, C, s, C, per, s).transpose(0, 3, 2, 4, 1, 5).reshape(n, B, D)

    bounds = (first_o, last_o)
    place = jnp.stack([g, c, z, f]).astype(jnp.int32)

    if direct:
        payload = pack(place, weight_rows, C, s, per, nb, bounds)
        parts = [payload[0]] + [hop(payload[d], d) for d in range(1, C)]
        pieces = [jnp.stack(parts)]
        for k in range(1, K):
            pieces.append(jnp.stack([cores(piece, k) for piece in parts]))
        slices = unpack(place, pieces, C, K, s, nb)
    else:
        full = lax.all_gather(weight_rows.astype(bf16), "fsdp", axis=0, tiled=True)
        rows_part = at(row_form(full), g, 1)
        cols_part = at(column_form(full), g, 1)
        slices = jnp.concatenate(
            [rows_part[:first_o], cols_part[first_o:last_o], rows_part[last_o:]], axis=0
        )
    part = D // C
    w_qkv = slices[:first_o].reshape(3 * part, D)
    w_o = (
        slices[first_o:last_o]
        .reshape(per, s, C, per, s)
        .transpose(0, 2, 1, 3, 4)
        .reshape(D, part)
    )
    up_end = last_o + hidden // B
    w_1 = slices[last_o:up_end].reshape(hidden // C, D)
    w_2 = slices[up_end:].reshape(hidden // C, D)

    vectors = vector_rows.astype(bf16).astype(f32)

    def own_features(vector):
        return at(vector.reshape(-1, C, s), g, 1).reshape(-1)

    def place_features(vector, count):
        spread = jnp.zeros((count // B, C, s), f32)
        return lax.dynamic_update_slice(
            spread, vector.reshape(count // B, 1, s), (0, g, 0)
        ).reshape(count)

    query_b, value_b = own_features(vectors[0]), own_features(vectors[1])
    out_b, gain_one, shift_one, down_b, gain_two, shift_two = [vectors[i] for i in range(2, 8)]
    up_b = own_features(vectors[8:].reshape(hidden))

    inputs = swap(tokens.reshape(T, D))
    cotan = swap(cotangent.reshape(T, D)).astype(f32)
    sequence = gather(inputs)
    S = C * T
    heads = part // HEAD_DIM
    score_scale = 1.0 / math.sqrt(HEAD_DIM)

    def split_heads(matrix):
        return matrix.reshape(S, heads, HEAD_DIM).transpose(1, 0, 2)

    def join_heads(stacked):
        return stacked.transpose(1, 0, 2).reshape(S, part)

    def batched(spec, left, right):
        return jnp.einsum(spec, left, right, preferred_element_type=f32)

    projected = mat_nt(sequence, w_qkv)
    query = split_heads((projected[:, :part] + query_b).astype(bf16))
    key = split_heads(projected[:, part : 2 * part].astype(bf16))
    value = split_heads((projected[:, 2 * part :] + value_b).astype(bf16))
    scores = batched("hqd,hkd->hqk", query, key) * score_scale
    top = jnp.max(scores, axis=-1, keepdims=True)
    log_total = top + jnp.log(jnp.sum(jnp.exp(scores - top), axis=-1, keepdims=True))
    probs = jnp.exp(scores - log_total)
    probs_b = probs.astype(bf16)
    attended_h = batched("hqk,hkd->hqd", probs_b, value).astype(bf16)
    attended = join_heads(attended_h)

    first_sum = inputs.astype(f32) + scatter(mat_nt(attended, w_o)) + out_b
    normed_one, inverse_one = normalize(first_sum)
    hidden_in = normed_one * gain_one + shift_one
    hidden_all = gather(hidden_in.astype(bf16))
    pre_act = mat_nt(hidden_all, w_1) + up_b
    cdf = 0.5 * (1.0 + lax.erf(pre_act * 0.7071067811865476))
    activ_b = (pre_act * cdf).astype(bf16)
    second_sum = hidden_in + scatter(mat_nn(activ_b, w_2)) + down_b
    normed_two, inverse_two = normalize(second_sum)
    output = swap_back((normed_two * gain_two + shift_two).astype(bf16))

    grad_gain_two = jnp.sum(cotan * normed_two, axis=0)
    grad_shift_two = jnp.sum(cotan, axis=0)
    grad_second = norm_back(cotan * gain_two, normed_two, inverse_two)
    grad_down_b = jnp.sum(grad_second, axis=0)
    grad_second_all = gather(grad_second.astype(bf16))
    grad_down_w = mat_tn(activ_b, grad_second_all)
    gelu_grad = cdf + pre_act * jnp.exp(-0.5 * pre_act * pre_act) * 0.3989422804014327
    grad_pre = mat_nt(grad_second_all, w_2) * gelu_grad
    grad_up_b = jnp.sum(grad_pre, axis=0)
    grad_pre_b = grad_pre.astype(bf16)
    grad_hidden = grad_second + scatter(mat_nn(grad_pre_b, w_1))
    grad_up_w = mat_tn(grad_pre_b, hidden_all)
    grad_gain_one = jnp.sum(grad_hidden * normed_one, axis=0)
    grad_shift_one = jnp.sum(grad_hidden, axis=0)
    grad_first = norm_back(grad_hidden * gain_one, normed_one, inverse_one)
    grad_out_b = jnp.sum(grad_first, axis=0)
    grad_first_all = gather(grad_first.astype(bf16))
    grad_out_w = mat_tn(grad_first_all, attended)
    grad_att = split_heads(mat_nn(grad_first_all, w_o).astype(bf16))

    delta = jnp.sum(grad_att.astype(f32) * attended_h.astype(f32), axis=-1, keepdims=True)
    grad_probs = batched("hqd,hkd->hqk", grad_att, value)
    grad_scores = (probs * (grad_probs - delta)).astype(bf16)
    grad_query = join_heads(batched("hqk,hkd->hqd", grad_scores, key) * score_scale)
    grad_key = join_heads(batched("hqk,hqd->hkd", grad_scores, query) * score_scale)
    grad_value = join_heads(batched("hqk,hqd->hkd", probs_b, grad_att))
    grad_proj = jnp.concatenate([grad_query, grad_key, grad_value], axis=1).astype(bf16)
    grad_qkv_w = mat_tn(grad_proj, sequence)
    grad_inputs = swap_back((grad_first + scatter(mat_nn(grad_proj, w_qkv))).astype(bf16))

    small = jnp.stack(
        [
            place_features(jnp.sum(grad_query, axis=0), D),
            place_features(jnp.sum(grad_value, axis=0), D),
            grad_out_b,
            grad_gain_one,
            grad_shift_one,
            grad_down_b,
            grad_gain_two,
            grad_shift_two,
        ]
    )
    vector_total = jnp.concatenate(
        [small, place_features(grad_up_b, hidden).reshape(-1, D)], axis=0
    )
    vector_total = all_sum(vector_total)
    new_vectors, new_vfirst, new_vsecond = adam_update(
        vector_rows, vector_total, vector_first, vector_second
    )

    grad_groups = [
        grad_qkv_w.reshape(3 * per, s, D),
        grad_out_w.reshape(per, C, s, per, s).transpose(0, 2, 1, 3, 4).reshape(per, s, D),
        grad_up_w.reshape(hidden // B, s, D),
        grad_down_w.reshape(hidden // B, s, D),
    ]
    if direct:
        reduced = jnp.concatenate([reduce_blocks(group) for group in grad_groups], axis=0)
        reduced = reduced.reshape(C, K * nb, C, s // K // C, D)
        arrived = [at(reduced, g)] + [hop(at(reduced, g ^ d), d) for d in range(1, C)]
        arrived = jnp.stack(arrived).reshape(C, K, nb, C, s // K // C, D)
        pieces = [at(arrived, c, 1)]
        for k in range(1, K):
            pieces.append(cores(at(arrived, (c + k) % K, 1), k))
        grad_out, weights_out, first_out, second_out = update(
            place, pieces, weight_rows, first_rows, second_rows, C, K, s, per, nb, bounds
        )
    else:
        spread = lax.dynamic_update_slice(
            jnp.zeros((blocks, C, s, D), bf16),
            jnp.concatenate(grad_groups, axis=0).astype(bf16)[:, None],
            (0, g, 0, 0),
        )
        matrix = jnp.where(
            ((jnp.arange(blocks) >= first_o) & (jnp.arange(blocks) < last_o))[:, None, None],
            from_column_form(spread),
            spread.reshape(blocks, B, D),
        ).reshape(total_rows, D)
        grad_out = lax.psum_scatter(matrix, "fsdp", scatter_dimension=0, tiled=True)
        grad_out = lax.psum(grad_out, "ctx").astype(f32)
        weights_out, first_out, second_out = adam_update(
            weight_rows, grad_out, first_rows, second_rows
        )
    return (
        output.reshape(1, T, D),
        grad_inputs.astype(f32).reshape(1, T, D),
        grad_out,
        weights_out,
        first_out,
        second_out,
        vector_total,
        new_vectors,
        new_vfirst,
        new_vsecond,
    )


def solution(mesh):
    shared = P()
    rows = P("fsdp", None)
    blocks = P("fsdp", "ctx", None)
    return jax.shard_map(
        local,
        mesh=mesh,
        in_specs=(blocks, blocks, rows, rows, rows, shared, shared, shared),
        out_specs=(blocks, blocks, rows, rows, rows, rows, shared, shared, shared, shared),
        check_vma=False,
    )
```
